32 devices in a mesh: row: 8 (over y, x, core), col: 4 (over z).
Axes of the slice: x: 2, y: 2, z: 4, core: 2. Of those that a mesh axis runs over, the one named last changes fastest.
Arguments:
- vector_panel: bfloat16 [8192, 256], P(('row', 'col')), may hold values from -6 to 6
- block_tiles: bfloat16 [3072, 128, 128], P(('row', 'col')), may hold values from -0.0625 to 0.0625
- tile_rows: int32 [3072], P(('row', 'col')), may hold values from 0 to 63, as said below
- tile_cols: int32 [3072], P(('row', 'col')), may hold values from 0 to 63, as said below
- owner_counts: int32 [32], P(('row', 'col')), may hold values from 1 to 96, as said below
Outputs:
- filtered: bfloat16 [8192, 256], P(('row', 'col'))
The draws below stay inside these ranges and needn't reach their ends.
Inputs may be any that keep to these rules, and one draw needn't show every extreme that they name: The live slots of owner (row index p, col index q) hold distinct pairs (tile_rows, tile_cols) with tile_rows <= tile_cols, tile_rows in p * 2 * 4 to (p + 1) * 2 * 4 - 1 and tile_cols // 2 % 4 = q; slots past the owner's count repeat its first pair and are ignored. `tile_cols`: see tile_rows. `owner_counts`: some owner fills all 96 slots.
All inputs are finite; a program needn't handle non-finite values.
Results may differ from the reference program's by a relative error of at most 0.022.
Values may be sent and summed in bfloat16 or wider, within the bound.
No kernel may reach another device: no remote copies, remote signals or barrier semaphores. Data moves between devices by JAX's collectives and lax.ppermute only.
A program may use at most 128 MiB of HBM per device.

```python
import jax
import jax.numpy as jnp
from jax import lax

BS = 128
W = 256
UB = 32
XB_DEV = 2
CAP = 96
NB = 64
ORBS = 8192
TILES = 3072
N_ROW = 8
N_COL = 4


def pattern(key):
    base = jax.random.fold_in(key, 11)
    key_score, key_factor, key_star = jax.random.split(base, 3)
    devices_all = N_ROW * N_COL
    device_ids = jnp.arange(devices_all, dtype=jnp.int32)
    row_owner = device_ids // N_COL
    col_owner = device_ids % N_COL
    range_blocks = XB_DEV * N_COL
    set_blocks = XB_DEV * N_ROW
    range_pos = jnp.arange(range_blocks, dtype=jnp.int32)
    set_pos = jnp.arange(set_blocks, dtype=jnp.int32)
    block_row = row_owner[:, None] * range_blocks + range_pos[None, :]
    block_col = (set_pos // XB_DEV)[None, :] * (N_COL * XB_DEV) + col_owner[:, None] * XB_DEV + (set_pos % XB_DEV)[None, :]
    pairs = range_blocks * set_blocks
    allowed = (block_row[:, :, None] <= block_col[:, None, :]).reshape(devices_all, pairs)
    ceiling = max(2, 2 ** 29 // pairs)
    pair_ids = jnp.arange(pairs, dtype=jnp.int32)
    scores = jax.random.randint(key_score, (devices_all, pairs), 0, ceiling, dtype=jnp.int32) * pairs + pair_ids[None, :]
    scores = jnp.where(allowed, scores, scores + 2 ** 30)
    corner = (device_ids[:, None] == 0) & (pair_ids[None, :] == 0) | (device_ids[:, None] == devices_all - 1) & (pair_ids[None, :] == pairs - 1)
    scores = jnp.where(corner, -1, scores)
    order = jnp.argsort(scores, axis=1, stable=True)[:, :CAP].astype(jnp.int32)
    valid_count = jnp.sum(allowed.astype(jnp.int32), axis=1)
    factor = jax.random.randint(key_factor, (devices_all,), 4, 9, dtype=jnp.int32)
    star = jax.random.randint(key_star, (), 0, N_COL, dtype=jnp.int32)
    factor = jnp.where(device_ids == star, 8, factor)
    target = CAP * (N_ROW - row_owner) * factor // (N_ROW * 8)
    counts = jnp.maximum(jnp.minimum(target, valid_count), 1).astype(jnp.int32)
    row_in = order // set_blocks
    set_in = order % set_blocks
    rows_all = jnp.take_along_axis(block_row, row_in, axis=1)
    cols_all = jnp.take_along_axis(block_col, set_in, axis=1)
    keep = jnp.arange(CAP, dtype=jnp.int32)[None, :] < counts[:, None]
    rows_all = jnp.where(keep, rows_all, rows_all[:, :1])
    cols_all = jnp.where(keep, cols_all, cols_all[:, :1])
    return (rows_all.reshape(-1).astype(jnp.int32), cols_all.reshape(-1).astype(jnp.int32), counts)


def draw_tile_rows(key, part):
    return pattern(key)[0]


def draw_tile_cols(key, part):
    return pattern(key)[1]


def draw_owner_counts(key, part):
    return pattern(key)[2]


def level_of(rng, dims, cuts, smallest, top_value):
    def one(axis_at, shards_of):
        steps = jax.random.uniform(jax.random.fold_in(jax.random.fold_in(rng, 6), axis_at), (shards_of,), jnp.float32, smallest / len(cuts), top_value / len(cuts))
        return jnp.repeat(jnp.exp(steps), dims[axis_at] // shards_of).reshape((-1,) + (1,) * (len(dims) - axis_at - 1))

    factor_of = one(*cuts[0])
    for cut in cuts[1:]:
        factor_of = factor_of * one(*cut)
    return factor_of


def scatter_about(stream_key, extent, scale, limit, pieces=(), kind=jnp.bfloat16):
    values = jax.random.normal(stream_key, extent, jnp.float32) * scale
    if len(pieces) > 0:
        values = level_of(stream_key, extent, pieces, -0.22, 0.18) * values
    return jnp.clip(values, min=-limit, max=limit).astype(kind)


def setup_inputs(seed: int = 0) -> dict:
    seeds = jax.random.split(jax.random.key(seed), 6)
    vector_panel = scatter_about(seeds[0], (ORBS, W), 1.0, 6.0, ((0, 32),))
    block_tiles = scatter_about(seeds[1], (TILES, BS, BS), (2 * UB * BS) ** -0.5, 0.0625, ((0, 32),))
    tile_rows = draw_tile_rows(jax.random.fold_in(seeds[5], 71), 0)
    tile_cols = draw_tile_cols(jax.random.fold_in(seeds[5], 71), 0)
    owner_counts = draw_owner_counts(jax.random.fold_in(seeds[5], 71), 0)
    return dict(vector_panel=vector_panel, block_tiles=block_tiles, tile_rows=tile_rows, tile_cols=tile_cols, owner_counts=owner_counts)


center_shift = 0.25
half_width = 1.25


def apply_blocks(panel_f, block_tiles, tile_rows, tile_cols, owner_counts):
    blocks = panel_f.reshape(NB, BS, W)
    range_count = XB_DEV * N_COL
    set_count = XB_DEV * N_ROW
    live_all = (jnp.arange(CAP, dtype=jnp.int32)[None, :] < owner_counts[:, None]).astype(jnp.float32)
    total = jnp.zeros((NB, BS, W), jnp.float32)
    range_ids = jnp.arange(range_count, dtype=jnp.int32)
    set_ids = jnp.arange(set_count, dtype=jnp.int32)

    def owner_step(owner, acc):
        owner = owner.astype(jnp.int32)
        row_owner = owner // N_COL
        col_owner = owner % N_COL
        start = (owner * CAP).astype(jnp.int32)
        tiles_f = lax.dynamic_slice_in_dim(block_tiles, start, CAP, 0).astype(jnp.float32)
        rows_here = lax.dynamic_slice_in_dim(tile_rows, start, CAP, 0)
        cols_here = lax.dynamic_slice_in_dim(tile_cols, start, CAP, 0)
        live = lax.dynamic_index_in_dim(live_all, owner, 0, keepdims=False)
        upper = jnp.einsum('sij,sjw->siw', tiles_f, blocks[cols_here], precision=lax.Precision.HIGHEST)
        lower = jnp.einsum('sji,sjw->siw', tiles_f, blocks[rows_here], precision=lax.Precision.HIGHEST)
        row_local = (rows_here - row_owner * range_count).astype(jnp.int32)
        set_local = ((cols_here // XB_DEV // N_COL) * XB_DEV + cols_here % XB_DEV).astype(jnp.int32)
        row_select = (row_local[None, :] == range_ids[:, None]).astype(jnp.float32) * live[None, :]
        set_select = (set_local[None, :] == set_ids[:, None]).astype(jnp.float32) * live[None, :]
        upper_sum = jnp.einsum('as,siw->aiw', row_select, upper, precision=lax.Precision.HIGHEST)
        lower_sum = jnp.einsum('bs,siw->biw', set_select, lower, precision=lax.Precision.HIGHEST)
        upper_sum = upper_sum.astype(jnp.bfloat16).astype(jnp.float32)
        lower_sum = lower_sum.astype(jnp.bfloat16).astype(jnp.float32)
        range_global = (row_owner * range_count + range_ids).astype(jnp.int32)
        set_global = ((set_ids // XB_DEV) * (N_COL * XB_DEV) + col_owner * XB_DEV + set_ids % XB_DEV).astype(jnp.int32)
        acc = acc.at[range_global].add(upper_sum)
        acc = acc.at[set_global].add(lower_sum)
        return acc

    total = lax.fori_loop(0, N_ROW * N_COL, owner_step, total)
    return total.reshape(NB * BS, W)


def reference(vector_panel, block_tiles, tile_rows, tile_cols, owner_counts):
    start_f = vector_panel.astype(jnp.float32)
    hx = apply_blocks(start_f, block_tiles, tile_rows, tile_cols, owner_counts)
    first_step = ((hx - center_shift * start_f) / half_width).astype(jnp.bfloat16)
    first_f = first_step.astype(jnp.float32)
    hfirst = apply_blocks(first_f, block_tiles, tile_rows, tile_cols, owner_counts)
    filtered = 2.0 * (hfirst - center_shift * first_f) / half_width - start_f
    return filtered.astype(jnp.bfloat16)
```

```python
import functools

import jax
import jax.numpy as jnp
from jax import lax
from jax.experimental import pallas as pl
from jax.experimental.pallas import tpu as pltpu
from jax.sharding import PartitionSpec as P

BS = 128
MIB = 2**20


center_shift = 0.25
half_width = 1.25


def power_of_two(n):
    return n & (n - 1) == 0


def densify_kernel(
    n_rows, n_cols, panel_blocks, rows_ref, cols_ref, count_ref, tiles_ref, a_ref, at_ref, table
):
    slots = tiles_ref.shape[0]
    range_blocks = panel_blocks * n_cols
    set_blocks = panel_blocks * n_rows
    p = lax.axis_index("row")
    q = lax.axis_index("col")

    def clear(i, carry):
        table[i] = slots
        return carry

    lax.fori_loop(0, range_blocks * set_blocks, clear, 0)

    def place(s, carry):
        row = rows_ref[s] - p * range_blocks
        row_at = ((row // panel_blocks) ^ q) * panel_blocks + row % panel_blocks
        col = cols_ref[s]
        relative = (col // (panel_blocks * n_cols)) ^ p
        unit = (relative % 2) * (n_rows // 2) + relative // 2
        col_at = unit * panel_blocks + col % panel_blocks
        table[row_at * set_blocks + col_at] = s
        return carry

    lax.fori_loop(0, jnp.minimum(count_ref[0], slots), place, 0)

    def fill(r, carry):
        for c in range(set_blocks):
            s = table[r * set_blocks + c]
            tile = tiles_ref[jnp.minimum(s, slots - 1)]
            tile = jnp.where(s < slots, tile, jnp.zeros_like(tile))
            a_ref[pl.ds(pl.multiple_of(r * BS, BS), BS), c * BS : (c + 1) * BS] = tile
            at_ref[c * BS : (c + 1) * BS, pl.ds(pl.multiple_of(r * BS, BS), BS)] = tile.T
        return carry

    lax.fori_loop(0, range_blocks, fill, 0)


def densify(n_rows, n_cols, panel_blocks, tile_rows, tile_cols, owner_counts, block_tiles):
    height = panel_blocks * n_cols * BS
    breadth = panel_blocks * n_rows * BS
    smem = pl.BlockSpec(memory_space=pltpu.SMEM)
    vmem = pl.BlockSpec(memory_space=pltpu.VMEM)
    return pl.pallas_call(
        functools.partial(densify_kernel, n_rows, n_cols, panel_blocks),
        out_shape=(
            jax.ShapeDtypeStruct((height, breadth), block_tiles.dtype),
            jax.ShapeDtypeStruct((breadth, height), block_tiles.dtype),
        ),
        in_specs=[smem, smem, smem, vmem],
        out_specs=(vmem, vmem),
        scratch_shapes=[pltpu.SMEM((height // BS * (breadth // BS),), jnp.int32)],
        compiler_params=pltpu.CompilerParams(vmem_limit_bytes=16 * MIB),
        cost_estimate=pl.CostEstimate(
            flops=0, transcendentals=0, bytes_accessed=2 * block_tiles.size + 4 * height * breadth
        ),
        name="densify",
    )(tile_rows, tile_cols, owner_counts, block_tiles)


def product_kernel(n_in, m_ref, *refs):
    panels, outs = refs[:n_in], refs[n_in:]
    done = 0
    for out in outs:
        for top in range(0, out.shape[0], 256):
            total = None
            at = 0
            for panel in panels:
                rows = panel.shape[0]
                term = jnp.dot(
                    m_ref[done : done + 256, at : at + rows],
                    panel[...],
                    preferred_element_type=jnp.float32,
                )
                total = term if total is None else total + term
                at += rows
            out[top : top + 256, :] = total.astype(out.dtype)
            done += 256


def product(matrix, panels, out_rows, name):
    width = panels[0].shape[1]
    vmem = pl.BlockSpec(memory_space=pltpu.VMEM)
    return pl.pallas_call(
        functools.partial(product_kernel, len(panels)),
        out_shape=tuple(jax.ShapeDtypeStruct((rows, width), jnp.bfloat16) for rows in out_rows),
        in_specs=[vmem] * (1 + len(panels)),
        out_specs=tuple(vmem for _ in out_rows),
        compiler_params=pltpu.CompilerParams(vmem_limit_bytes=16 * MIB),
        cost_estimate=pl.CostEstimate(
            flops=2 * matrix.size * width,
            transcendentals=0,
            bytes_accessed=2 * (matrix.size + sum(matrix.shape) * width),
        ),
        name=name,
    )(matrix, *panels)


def swap(x, axis, j):
    return lax.ppermute(x, axis, [(i, i ^ j) for i in range(lax.axis_size(axis))])


def apply_dense(panel, matrix, matrix_t):
    n_rows = lax.axis_size("row")
    n_cols = lax.axis_size("col")
    rows, width = panel.shape
    range_panels = [panel] + [swap(panel, "col", j) for j in range(1, n_cols)]
    near = [panel] + [swap(panel, "row", j) for j in range(2, n_rows, 2)]
    far = swap(jnp.concatenate(near), "row", 1)
    upper = product(matrix, near + [far], [rows] * n_cols, "upper")
    own = upper[0].astype(jnp.float32)
    for j in range(1, n_cols):
        own += swap(upper[j], "col", j).astype(jnp.float32)
    half = n_rows // 2
    keep, give = product(matrix_t, range_panels, [half * rows] * 2, "lower")
    paired = keep.astype(jnp.float32) + swap(give, "row", 1).astype(jnp.float32)
    paired = paired.reshape(half, rows, width)
    own += paired[0]
    for k in range(1, half):
        own += swap(paired[k].astype(jnp.bfloat16), "row", 2 * k).astype(jnp.float32)
    return own


def apply_slots(
    panel, block_tiles, row_slot, set_slot, row_select, set_select, range_blocks, set_blocks
):
    width = panel.shape[1]
    gathered_set = lax.all_gather(panel, "row", axis=0, tiled=True).reshape(set_blocks, BS, width)
    picked_set = jnp.take(gathered_set, set_slot, axis=0)
    upper = jnp.einsum("sij,sjw->siw", block_tiles, picked_set, preferred_element_type=jnp.float32)
    upper_sum = jnp.einsum(
        "as,siw->aiw", row_select, upper, precision=lax.Precision.HIGHEST
    ).astype(jnp.bfloat16)
    own_upper = lax.psum_scatter(
        upper_sum.reshape(range_blocks * BS, width), "col", scatter_dimension=0, tiled=True
    ).astype(jnp.float32)
    gathered_range = lax.all_gather(panel, "col", axis=0, tiled=True).reshape(
        range_blocks, BS, width
    )
    picked_range = jnp.take(gathered_range, row_slot, axis=0)
    lower = jnp.einsum(
        "sji,sjw->siw", block_tiles, picked_range, preferred_element_type=jnp.float32
    )
    lower_sum = jnp.einsum(
        "bs,siw->biw", set_select, lower, precision=lax.Precision.HIGHEST
    ).astype(jnp.bfloat16)
    own_lower = lax.psum_scatter(
        lower_sum.reshape(set_blocks * BS, width), "row", scatter_dimension=0, tiled=True
    ).astype(jnp.float32)
    return own_upper + own_lower


def slot_operator(panel_blocks, block_tiles, tile_rows, tile_cols, owner_counts):
    n_rows = lax.axis_size("row")
    n_cols = lax.axis_size("col")
    row_index = lax.axis_index("row")
    slots = block_tiles.shape[0]
    range_blocks = panel_blocks * n_cols
    set_blocks = panel_blocks * n_rows
    row_slot = tile_rows - row_index * range_blocks
    shard_of = tile_cols // panel_blocks
    set_slot = shard_of // n_cols * panel_blocks + tile_cols % panel_blocks
    live_slots = jnp.arange(slots, dtype=jnp.int32) < owner_counts[0]
    row_select = (
        (row_slot[None, :] == jnp.arange(range_blocks, dtype=jnp.int32)[:, None])
        & live_slots[None, :]
    ).astype(jnp.float32)
    set_select = (
        (set_slot[None, :] == jnp.arange(set_blocks, dtype=jnp.int32)[:, None])
        & live_slots[None, :]
    ).astype(jnp.float32)

    def operate(panel):
        return apply_slots(
            panel, block_tiles, row_slot, set_slot, row_select, set_select, range_blocks, set_blocks
        )

    return operate


def per_device(vector_panel, block_tiles, tile_rows, tile_cols, owner_counts):
    n_rows = lax.axis_size("row")
    n_cols = lax.axis_size("col")
    panel_blocks = vector_panel.shape[0] // BS
    pairs = panel_blocks * n_cols * panel_blocks * n_rows
    dense = (
        power_of_two(n_rows)
        and power_of_two(n_cols)
        and n_rows >= 2
        and panel_blocks % 2 == 0
        and pairs <= 2 * block_tiles.shape[0]
    )
    if dense:
        matrix, matrix_t = densify(
            n_rows, n_cols, panel_blocks, tile_rows, tile_cols, owner_counts, block_tiles
        )
        operate = functools.partial(apply_dense, matrix=matrix, matrix_t=matrix_t)
    else:
        operate = slot_operator(panel_blocks, block_tiles, tile_rows, tile_cols, owner_counts)

    start_f = vector_panel.astype(jnp.float32)
    hx = operate(vector_panel)
    first_step = ((hx - center_shift * start_f) / half_width).astype(jnp.bfloat16)
    first_f = first_step.astype(jnp.float32)
    hfirst = operate(first_step)
    filtered = 2.0 * (hfirst - center_shift * first_f) / half_width - start_f
    return filtered.astype(jnp.bfloat16)


def solution(mesh):
    in_specs = (
        P(("row", "col"), None),
        P(("row", "col"), None, None),
        P(("row", "col")),
        P(("row", "col")),
        P(("row", "col")),
    )
    out_specs = P(("row", "col"), None)
    return jax.shard_map(
        per_device, mesh=mesh, in_specs=in_specs, out_specs=out_specs, check_vma=False
    )
```

```python
import functools

import jax
import jax.numpy as jnp
from jax import lax
from jax.experimental import pallas as pl
from jax.experimental.pallas import tpu as pltpu
from jax.sharding import PartitionSpec as P


BS = 128
MIB = 2**20


center_shift = 0.25
half_width = 1.25


def power_of_two(n):
    return n & (n - 1) == 0


def densify_kernel(
    n_rows, n_cols, panel_blocks, rows_ref, cols_ref, count_ref, tiles_ref, a_ref, at_ref, table
):
    slots = tiles_ref.shape[0]
    range_blocks = panel_blocks * n_cols
    set_blocks = panel_blocks * n_rows
    p = lax.axis_index("row")
    q = lax.axis_index("col")

    def clear(i, carry):
        table[i] = slots
        return carry

    lax.fori_loop(0, range_blocks * set_blocks, clear, 0)

    def place(s, carry):
        row = rows_ref[s] - p * range_blocks
        row_at = ((row // panel_blocks) ^ q) * panel_blocks + row % panel_blocks
        col = cols_ref[s]
        relative = (col // (panel_blocks * n_cols)) ^ p
        unit = (relative % 2) * (n_rows // 2) + relative // 2
        col_at = unit * panel_blocks + col % panel_blocks
        table[row_at * set_blocks + col_at] = s
        return carry

    lax.fori_loop(0, jnp.minimum(count_ref[0], slots), place, 0)

    def fill(r, carry):
        for c in range(set_blocks):
            s = table[r * set_blocks + c]
            tile = tiles_ref[jnp.minimum(s, slots - 1)]
            tile = jnp.where(s < slots, tile, jnp.zeros_like(tile))
            a_ref[pl.ds(pl.multiple_of(r * BS, BS), BS), c * BS : (c + 1) * BS] = tile
            at_ref[c * BS : (c + 1) * BS, pl.ds(pl.multiple_of(r * BS, BS), BS)] = tile.T
        return carry

    lax.fori_loop(0, range_blocks, fill, 0)


def densify(n_rows, n_cols, panel_blocks, tile_rows, tile_cols, owner_counts, block_tiles):
    height = panel_blocks * n_cols * BS
    breadth = panel_blocks * n_rows * BS
    smem = pl.BlockSpec(memory_space=pltpu.SMEM)
    vmem = pl.BlockSpec(memory_space=pltpu.VMEM)
    return pl.pallas_call(
        functools.partial(densify_kernel, n_rows, n_cols, panel_blocks),
        out_shape=(
            jax.ShapeDtypeStruct((height, breadth), block_tiles.dtype),
            jax.ShapeDtypeStruct((breadth, height), block_tiles.dtype),
        ),
        in_specs=[smem, smem, smem, vmem],
        out_specs=(vmem, vmem),
        scratch_shapes=[pltpu.SMEM((height // BS * (breadth // BS),), jnp.int32)],
        compiler_params=pltpu.CompilerParams(vmem_limit_bytes=16 * MIB),
        cost_estimate=pl.CostEstimate(
            flops=0, transcendentals=0, bytes_accessed=2 * block_tiles.size + 4 * height * breadth
        ),
        name="densify",
    )(tile_rows, tile_cols, owner_counts, block_tiles)


def product_kernel(n_in, m_ref, *refs):
    panels, outs = refs[:n_in], refs[n_in:]
    done = 0
    for out in outs:
        for top in range(0, out.shape[0], 256):
            total = None
            at = 0
            for panel in panels:
                rows = panel.shape[0]
                term = jnp.dot(
                    m_ref[done : done + 256, at : at + rows],
                    panel[...],
                    preferred_element_type=jnp.float32,
                )
                total = term if total is None else total + term
                at += rows
            out[top : top + 256, :] = total.astype(out.dtype)
            done += 256


def product(matrix, panels, out_rows):
    width = panels[0].shape[1]
    vmem = pl.BlockSpec(memory_space=pltpu.VMEM)
    return pl.pallas_call(
        functools.partial(product_kernel, len(panels)),
        out_shape=tuple(jax.ShapeDtypeStruct((rows, width), jnp.bfloat16) for rows in out_rows),
        in_specs=[vmem] * (1 + len(panels)),
        out_specs=tuple(vmem for _ in out_rows),
        compiler_params=pltpu.CompilerParams(vmem_limit_bytes=16 * MIB),
        cost_estimate=pl.CostEstimate(
            flops=2 * matrix.size * width,
            transcendentals=0,
            bytes_accessed=2 * (matrix.size + sum(matrix.shape) * width),
        ),
    )(matrix, *panels)


def swap(x, axis, j):
    return lax.ppermute(x, axis, [(i, i ^ j) for i in range(lax.axis_size(axis))])


def apply_dense(panel, matrix, matrix_t):
    n_rows = lax.axis_size("row")
    n_cols = lax.axis_size("col")
    rows, width = panel.shape
    half = n_rows // 2
    range_panels = [panel] + [swap(panel, "col", j) for j in range(1, n_cols)]
    near = [panel] + [swap(panel, "row", 2 * k) for k in range(1, half)]
    far = swap(jnp.concatenate(near), "row", 1)
    upper = product(matrix, near + [far], [rows] * n_cols)
    own = upper[0].astype(jnp.float32)
    for j in range(1, n_cols):
        own += swap(upper[j], "col", j).astype(jnp.float32)
    keep, give = product(matrix_t, range_panels, [half * rows] * 2)
    paired = keep.astype(jnp.float32) + swap(give, "row", 1).astype(jnp.float32)
    paired = paired.reshape(half, rows, width)
    own += paired[0]
    for k in range(1, half):
        share = paired[k].astype(jnp.bfloat16)
        own += swap(share, "row", 2 * k).astype(jnp.float32)
    return own


def apply_slots(
    panel, block_tiles, row_slot, set_slot, row_select, set_select, range_blocks, set_blocks
):
    width = panel.shape[1]
    gathered_set = lax.all_gather(panel, "row", axis=0, tiled=True).reshape(set_blocks, BS, width)
    picked_set = jnp.take(gathered_set, set_slot, axis=0)
    upper = jnp.einsum("sij,sjw->siw", block_tiles, picked_set, preferred_element_type=jnp.float32)
    upper_sum = jnp.einsum(
        "as,siw->aiw", row_select, upper, precision=lax.Precision.HIGHEST
    ).astype(jnp.bfloat16)
    own_upper = lax.psum_scatter(
        upper_sum.reshape(range_blocks * BS, width), "col", scatter_dimension=0, tiled=True
    ).astype(jnp.float32)
    gathered_range = lax.all_gather(panel, "col", axis=0, tiled=True).reshape(
        range_blocks, BS, width
    )
    picked_range = jnp.take(gathered_range, row_slot, axis=0)
    lower = jnp.einsum(
        "sji,sjw->siw", block_tiles, picked_range, preferred_element_type=jnp.float32
    )
    lower_sum = jnp.einsum(
        "bs,siw->biw", set_select, lower, precision=lax.Precision.HIGHEST
    ).astype(jnp.bfloat16)
    own_lower = lax.psum_scatter(
        lower_sum.reshape(set_blocks * BS, width), "row", scatter_dimension=0, tiled=True
    ).astype(jnp.float32)
    return own_upper + own_lower


def slot_operator(panel_blocks, block_tiles, tile_rows, tile_cols, owner_counts):
    n_rows = lax.axis_size("row")
    n_cols = lax.axis_size("col")
    row_index = lax.axis_index("row")
    slots = block_tiles.shape[0]
    range_blocks = panel_blocks * n_cols
    set_blocks = panel_blocks * n_rows
    row_slot = tile_rows - row_index * range_blocks
    shard_of = tile_cols // panel_blocks
    set_slot = shard_of // n_cols * panel_blocks + tile_cols % panel_blocks
    live_slots = jnp.arange(slots, dtype=jnp.int32) < owner_counts[0]
    row_select = (
        (row_slot[None, :] == jnp.arange(range_blocks, dtype=jnp.int32)[:, None])
        & live_slots[None, :]
    ).astype(jnp.float32)
    set_select = (
        (set_slot[None, :] == jnp.arange(set_blocks, dtype=jnp.int32)[:, None])
        & live_slots[None, :]
    ).astype(jnp.float32)

    def operate(panel):
        return apply_slots(
            panel, block_tiles, row_slot, set_slot, row_select, set_select, range_blocks, set_blocks
        )

    return operate


def is_dense(n_rows, n_cols, panel_blocks, slots):
    return (
        power_of_two(n_rows)
        and power_of_two(n_cols)
        and n_rows >= 4
        and n_cols >= 2
        and panel_blocks % 2 == 0
        and panel_blocks * n_cols * panel_blocks * n_rows <= 2 * slots
    )


def per_device(vector_panel, block_tiles, tile_rows, tile_cols, owner_counts):
    n_rows = lax.axis_size("row")
    n_cols = lax.axis_size("col")
    panel_blocks = vector_panel.shape[0] // BS
    if is_dense(n_rows, n_cols, panel_blocks, block_tiles.shape[0]):
        matrix, matrix_t = densify(
            n_rows, n_cols, panel_blocks, tile_rows, tile_cols, owner_counts, block_tiles
        )
        operate = functools.partial(apply_dense, matrix=matrix, matrix_t=matrix_t)
    else:
        operate = slot_operator(panel_blocks, block_tiles, tile_rows, tile_cols, owner_counts)

    start_f = vector_panel.astype(jnp.float32)
    hx = operate(vector_panel)
    first_step = ((hx - center_shift * start_f) / half_width).astype(jnp.bfloat16)
    first_f = first_step.astype(jnp.float32)
    hfirst = operate(first_step)
    filtered = 2.0 * (hfirst - center_shift * first_f) / half_width - start_f
    return filtered.astype(jnp.bfloat16)


def solution(mesh):
    in_specs = (
        P(("row", "col"), None),
        P(("row", "col"), None, None),
        P(("row", "col")),
        P(("row", "col")),
        P(("row", "col")),
    )
    out_specs = P(("row", "col"), None)
    step = jax.shard_map(
        per_device, mesh=mesh, in_specs=in_specs, out_specs=out_specs, check_vma=False
    )

    def run(vector_panel, block_tiles, tile_rows, tile_cols, owner_counts):
        args = (vector_panel, block_tiles, tile_rows, tile_cols, owner_counts)
        return step(*args)

    return run
```

```python
import functools

import jax
import jax.numpy as jnp
from jax import lax
from jax.experimental import pallas as pl
from jax.experimental.pallas import tpu as pltpu
from jax.sharding import PartitionSpec as P


BS = 128
MIB = 2**20


center_shift = 0.25
half_width = 1.25


def power_of_two(n):
    return n & (n - 1) == 0


def densify_kernel(
    n_rows,
    n_cols,
    panel_blocks,
    rows_hbm,
    cols_hbm,
    count_hbm,
    tiles_hbm,
    a_ref,
    at_ref,
    rows_ref,
    cols_ref,
    count_ref,
    tiles_ref,
    table,
    sems,
):
    slots = tiles_ref.shape[0]
    range_blocks = panel_blocks * n_cols
    set_blocks = panel_blocks * n_rows
    p = lax.axis_index("row")
    q = lax.axis_index("col")
    moves = [
        pltpu.make_async_copy(src, dst, sems.at[i])
        for i, (src, dst) in enumerate(
            (
                (rows_hbm, rows_ref),
                (cols_hbm, cols_ref),
                (count_hbm, count_ref),
                (tiles_hbm, tiles_ref),
            )
        )
    ]
    for move in moves:
        move.start()

    def clear(r, carry):
        for c in range(set_blocks):
            table[r * set_blocks + c] = slots
        return carry

    lax.fori_loop(0, range_blocks, clear, 0)
    for move in moves[:3]:
        move.wait()

    def place(s, carry):
        row = rows_ref[s] - p * range_blocks
        row_at = ((row // panel_blocks) ^ q) * panel_blocks + row % panel_blocks
        col = cols_ref[s]
        relative = (col // (panel_blocks * n_cols)) ^ p
        unit = (relative % 2) * (n_rows // 2) + relative // 2
        col_at = unit * panel_blocks + col % panel_blocks
        table[row_at * set_blocks + col_at] = s
        return carry

    lax.fori_loop(0, jnp.minimum(count_ref[0], slots), place, 0)
    moves[3].wait()

    def fill(r, carry):
        for c in range(set_blocks):
            s = table[r * set_blocks + c]
            tile = tiles_ref[jnp.minimum(s, slots - 1)]
            tile = jnp.where(s < slots, tile, jnp.zeros_like(tile))
            a_ref[pl.ds(pl.multiple_of(r * BS, BS), BS), c * BS : (c + 1) * BS] = tile
            at_ref[c * BS : (c + 1) * BS, pl.ds(pl.multiple_of(r * BS, BS), BS)] = tile.T
        return carry

    lax.fori_loop(0, range_blocks, fill, 0)


def densify(n_rows, n_cols, panel_blocks, tile_rows, tile_cols, owner_counts, block_tiles):
    height = panel_blocks * n_cols * BS
    breadth = panel_blocks * n_rows * BS
    hbm = pl.BlockSpec(memory_space=pltpu.HBM)
    vmem = pl.BlockSpec(memory_space=pltpu.VMEM)
    return pl.pallas_call(
        functools.partial(densify_kernel, n_rows, n_cols, panel_blocks),
        out_shape=(
            jax.ShapeDtypeStruct((height, breadth), block_tiles.dtype),
            jax.ShapeDtypeStruct((breadth, height), block_tiles.dtype),
        ),
        in_specs=[hbm] * 4,
        out_specs=(vmem, vmem),
        scratch_shapes=[
            pltpu.SMEM(tile_rows.shape, jnp.int32),
            pltpu.SMEM(tile_cols.shape, jnp.int32),
            pltpu.SMEM(owner_counts.shape, jnp.int32),
            pltpu.VMEM(block_tiles.shape, block_tiles.dtype),
            pltpu.SMEM((height // BS * (breadth // BS),), jnp.int32),
            pltpu.SemaphoreType.DMA((4,)),
        ],
        compiler_params=pltpu.CompilerParams(vmem_limit_bytes=20 * MIB),
        cost_estimate=pl.CostEstimate(
            flops=0, transcendentals=0, bytes_accessed=2 * block_tiles.size + 4 * height * breadth
        ),
        name="densify",
    )(tile_rows, tile_cols, owner_counts, block_tiles)


def product_kernel(n_in, start, m_ref, *refs):
    panels, outs = refs[:n_in], refs[n_in:]
    done = start
    for out in outs:
        for top in range(0, out.shape[0], 256):
            total = None
            at = 0
            for panel in panels:
                rows = panel.shape[0]
                term = jnp.dot(
                    m_ref[done : done + 256, at : at + rows],
                    panel[...],
                    preferred_element_type=jnp.float32,
                )
                total = term if total is None else total + term
                at += rows
            out[top : top + 256, :] = total.astype(out.dtype)
            done += 256


def product(matrix, panels, start, out_rows):
    width = panels[0].shape[1]
    vmem = pl.BlockSpec(memory_space=pltpu.VMEM)
    return pl.pallas_call(
        functools.partial(product_kernel, len(panels), start),
        out_shape=tuple(jax.ShapeDtypeStruct((rows, width), jnp.bfloat16) for rows in out_rows),
        in_specs=[vmem] * (1 + len(panels)),
        out_specs=tuple(vmem for _ in out_rows),
        compiler_params=pltpu.CompilerParams(vmem_limit_bytes=16 * MIB),
        cost_estimate=pl.CostEstimate(
            flops=2 * sum(out_rows) * matrix.shape[1] * width,
            transcendentals=0,
            bytes_accessed=2 * (sum(out_rows) * (matrix.shape[1] + width) + matrix.shape[1] * width),
        ),
    )(matrix, *panels)


def swap(x, axis, j):
    return lax.ppermute(x, axis, [(i, i ^ j) for i in range(lax.axis_size(axis))])


def apply_dense(panel, matrix, matrix_t):
    n_rows = lax.axis_size("row")
    n_cols = lax.axis_size("col")
    rows, width = panel.shape
    half = n_rows // 2
    range_panels = [panel] + [swap(panel, "col", j) for j in range(1, n_cols)]
    near = [panel] + [swap(panel, "row", 2 * k) for k in range(1, half)]
    far = swap(jnp.concatenate(near), "row", 1)
    upper = product(matrix, near + [far], 0, [rows] * n_cols)
    own = upper[0].astype(jnp.float32)
    for j in range(1, n_cols):
        own += swap(upper[j], "col", j).astype(jnp.float32)
    (give,) = product(matrix_t, range_panels, half * rows, [half * rows])
    (keep,) = product(matrix_t, range_panels, 0, [half * rows])
    paired = keep.astype(jnp.float32) + swap(give, "row", 1).astype(jnp.float32)
    paired = paired.reshape(half, rows, width)
    own += paired[0]
    for k in range(1, half):
        share = paired[k].astype(jnp.bfloat16)
        own += swap(share, "row", 2 * k).astype(jnp.float32)
    return own


def apply_slots(
    panel, block_tiles, row_slot, set_slot, row_select, set_select, range_blocks, set_blocks
):
    width = panel.shape[1]
    gathered_set = lax.all_gather(panel, "row", axis=0, tiled=True).reshape(set_blocks, BS, width)
    picked_set = jnp.take(gathered_set, set_slot, axis=0)
    upper = jnp.einsum("sij,sjw->siw", block_tiles, picked_set, preferred_element_type=jnp.float32)
    upper_sum = jnp.einsum(
        "as,siw->aiw", row_select, upper, precision=lax.Precision.HIGHEST
    ).astype(jnp.bfloat16)
    own_upper = lax.psum_scatter(
        upper_sum.reshape(range_blocks * BS, width), "col", scatter_dimension=0, tiled=True
    ).astype(jnp.float32)
    gathered_range = lax.all_gather(panel, "col", axis=0, tiled=True).reshape(
        range_blocks, BS, width
    )
    picked_range = jnp.take(gathered_range, row_slot, axis=0)
    lower = jnp.einsum(
        "sji,sjw->siw", block_tiles, picked_range, preferred_element_type=jnp.float32
    )
    lower_sum = jnp.einsum(
        "bs,siw->biw", set_select, lower, precision=lax.Precision.HIGHEST
    ).astype(jnp.bfloat16)
    own_lower = lax.psum_scatter(
        lower_sum.reshape(set_blocks * BS, width), "row", scatter_dimension=0, tiled=True
    ).astype(jnp.float32)
    return own_upper + own_lower


def slot_operator(panel_blocks, block_tiles, tile_rows, tile_cols, owner_counts):
    n_rows = lax.axis_size("row")
    n_cols = lax.axis_size("col")
    row_index = lax.axis_index("row")
    slots = block_tiles.shape[0]
    range_blocks = panel_blocks * n_cols
    set_blocks = panel_blocks * n_rows
    row_slot = tile_rows - row_index * range_blocks
    shard_of = tile_cols // panel_blocks
    set_slot = shard_of // n_cols * panel_blocks + tile_cols % panel_blocks
    live_slots = jnp.arange(slots, dtype=jnp.int32) < owner_counts[0]
    row_select = (
        (row_slot[None, :] == jnp.arange(range_blocks, dtype=jnp.int32)[:, None])
        & live_slots[None, :]
    ).astype(jnp.float32)
    set_select = (
        (set_slot[None, :] == jnp.arange(set_blocks, dtype=jnp.int32)[:, None])
        & live_slots[None, :]
    ).astype(jnp.float32)

    def operate(panel):
        return apply_slots(
            panel, block_tiles, row_slot, set_slot, row_select, set_select, range_blocks, set_blocks
        )

    return operate


def is_dense(n_rows, n_cols, panel_blocks, slots):
    return (
        power_of_two(n_rows)
        and power_of_two(n_cols)
        and n_rows >= 4
        and n_cols >= 2
        and panel_blocks % 2 == 0
        and panel_blocks * n_cols * panel_blocks * n_rows <= 2 * slots
    )


def per_device(vector_panel, block_tiles, tile_rows, tile_cols, owner_counts):
    n_rows = lax.axis_size("row")
    n_cols = lax.axis_size("col")
    panel_blocks = vector_panel.shape[0] // BS
    if is_dense(n_rows, n_cols, panel_blocks, block_tiles.shape[0]):
        matrix, matrix_t = densify(
            n_rows, n_cols, panel_blocks, tile_rows, tile_cols, owner_counts, block_tiles
        )
        operate = functools.partial(apply_dense, matrix=matrix, matrix_t=matrix_t)
    else:
        operate = slot_operator(panel_blocks, block_tiles, tile_rows, tile_cols, owner_counts)

    start_f = vector_panel.astype(jnp.float32)
    hx = operate(vector_panel)
    first_step = ((hx - center_shift * start_f) / half_width).astype(jnp.bfloat16)
    first_f = first_step.astype(jnp.float32)
    hfirst = operate(first_step)
    filtered = 2.0 * (hfirst - center_shift * first_f) / half_width - start_f
    return filtered.astype(jnp.bfloat16)


def solution(mesh):
    in_specs = (
        P(("row", "col"), None),
        P(("row", "col"), None, None),
        P(("row", "col")),
        P(("row", "col")),
        P(("row", "col")),
    )
    out_specs = P(("row", "col"), None)
    step = jax.shard_map(
        per_device, mesh=mesh, in_specs=in_specs, out_specs=out_specs, check_vma=False
    )

    def run(vector_panel, block_tiles, tile_rows, tile_cols, owner_counts):
        args = (vector_panel, block_tiles, tile_rows, tile_cols, owner_counts)
        return step(*args)

    return run
```

```python
import functools

import jax
import jax.numpy as jnp
from jax import lax
from jax.experimental import pallas as pl
from jax.experimental.pallas import tpu as pltpu
from jax.sharding import PartitionSpec as P


BS = 128
MIB = 2**20


center_shift = 0.25
half_width = 1.25


def power_of_two(n):
    return n & (n - 1) == 0


def slot_table(n_rows, n_cols, panel_blocks, tile_rows, tile_cols, owner_counts):
    slots = tile_rows.shape[0]
    range_blocks = panel_blocks * n_cols
    set_blocks = panel_blocks * n_rows
    p = lax.axis_index("row")
    q = lax.axis_index("col")
    row = tile_rows - p * range_blocks
    row_at = ((row // panel_blocks) ^ q) * panel_blocks + row % panel_blocks
    relative = (tile_cols // range_blocks) ^ p
    unit = (relative % 2) * (n_rows // 2) + relative // 2
    place = row_at * set_blocks + unit * panel_blocks + tile_cols % panel_blocks
    slot = jnp.arange(slots, dtype=jnp.int32)
    place = jnp.where(slot < owner_counts[0], place, -1)
    blocks = jnp.arange(range_blocks * set_blocks, dtype=jnp.int32)
    return jnp.min(jnp.where(place[None, :] == blocks[:, None], slot[None, :], slots), axis=1)


def densify_kernel(table, tiles_ref, a_ref):
    slots = tiles_ref.shape[0]
    set_blocks = a_ref.shape[1] // BS

    def fill(r, carry):
        for c in range(set_blocks):
            s = table[r * set_blocks + c]
            tile = tiles_ref[jnp.minimum(s, slots - 1)]
            tile = jnp.where(s < slots, tile, jnp.zeros_like(tile))
            a_ref[pl.ds(pl.multiple_of(r * BS, BS), BS), c * BS : (c + 1) * BS] = tile
        return carry

    lax.fori_loop(0, a_ref.shape[0] // BS, fill, 0)


def densify(height, breadth, table, block_tiles):
    vmem = pl.BlockSpec(memory_space=pltpu.VMEM)
    return pl.pallas_call(
        densify_kernel,
        out_shape=jax.ShapeDtypeStruct((height, breadth), block_tiles.dtype),
        in_specs=[pl.BlockSpec(memory_space=pltpu.SMEM), vmem],
        out_specs=vmem,
        compiler_params=pltpu.CompilerParams(vmem_limit_bytes=16 * MIB),
        cost_estimate=pl.CostEstimate(
            flops=0, transcendentals=0, bytes_accessed=2 * (block_tiles.size + height * breadth)
        ),
        name="densify",
    )(table, block_tiles)


def transpose_kernel(a_ref, at_ref):
    def fill(r, carry):
        rows = pl.ds(pl.multiple_of(r * BS, BS), BS)
        for c in range(a_ref.shape[1] // BS):
            at_ref[c * BS : (c + 1) * BS, rows] = a_ref[rows, c * BS : (c + 1) * BS].T
        return carry

    lax.fori_loop(0, a_ref.shape[0] // BS, fill, 0)


def transpose(matrix):
    height, breadth = matrix.shape
    vmem = pl.BlockSpec(memory_space=pltpu.VMEM)
    return pl.pallas_call(
        transpose_kernel,
        out_shape=jax.ShapeDtypeStruct((breadth, height), matrix.dtype),
        in_specs=[vmem],
        out_specs=vmem,
        compiler_params=pltpu.CompilerParams(vmem_limit_bytes=16 * MIB),
        cost_estimate=pl.CostEstimate(
            flops=0, transcendentals=0, bytes_accessed=4 * height * breadth
        ),
        name="mirror",
    )(matrix)


def product_kernel(n_in, start, m_ref, *refs):
    panels, outs = refs[:n_in], refs[n_in:]
    done = start
    for out in outs:
        for top in range(0, out.shape[0], 256):
            total = None
            at = 0
            for panel in panels:
                rows = panel.shape[0]
                term = jnp.dot(
                    m_ref[done : done + 256, at : at + rows],
                    panel[...],
                    preferred_element_type=jnp.float32,
                )
                total = term if total is None else total + term
                at += rows
            out[top : top + 256, :] = total.astype(out.dtype)
            done += 256


def product(matrix, panels, start, out_rows):
    width = panels[0].shape[1]
    vmem = pl.BlockSpec(memory_space=pltpu.VMEM)
    return pl.pallas_call(
        functools.partial(product_kernel, len(panels), start),
        out_shape=tuple(jax.ShapeDtypeStruct((rows, width), jnp.bfloat16) for rows in out_rows),
        in_specs=[vmem] * (1 + len(panels)),
        out_specs=tuple(vmem for _ in out_rows),
        compiler_params=pltpu.CompilerParams(vmem_limit_bytes=16 * MIB),
        cost_estimate=pl.CostEstimate(
            flops=2 * sum(out_rows) * matrix.shape[1] * width,
            transcendentals=0,
            bytes_accessed=2 * (sum(out_rows) * (matrix.shape[1] + width) + matrix.shape[1] * width),
        ),
    )(matrix, *panels)


def swap(x, axis, j):
    return lax.ppermute(x, axis, [(i, i ^ j) for i in range(lax.axis_size(axis))])


def hops(j):
    masks = []
    while j:
        masks.append((1 << j.bit_length()) - 1)
        j ^= masks[-1]
    return masks


def apply_dense(panel, matrix, matrix_t):
    n_rows = lax.axis_size("row")
    n_cols = lax.axis_size("col")
    rows, width = panel.shape
    half = n_rows // 2
    by_hops = sorted(range(1, n_cols), key=lambda j: (len(hops(j)), -j))

    range_panels = [panel] + [None] * (n_cols - 1)
    for j in by_hops:
        last = hops(j)[-1]
        range_panels[j] = swap(range_panels[j ^ last], "col", last)
    near = [panel] + [swap(panel, "row", 2 * k) for k in range(1, half)]
    far = swap(jnp.concatenate(near), "row", 1)
    upper = list(product(matrix, near + [far], 0, [rows] * n_cols))
    for j in reversed(by_hops):
        last = hops(j)[-1]
        part = swap(upper[j].astype(jnp.bfloat16), "col", last)
        upper[j ^ last] = upper[j ^ last].astype(jnp.float32) + part.astype(jnp.float32)
    own = upper[0].astype(jnp.float32)
    (give,) = product(matrix_t, range_panels, half * rows, [half * rows])
    (keep,) = product(matrix_t, range_panels, 0, [half * rows])
    paired = keep.astype(jnp.float32) + swap(give, "row", 1).astype(jnp.float32)
    paired = paired.reshape(half, rows, width)
    own += paired[0]
    for k in range(1, half):
        share = paired[k].astype(jnp.bfloat16)
        own += swap(share, "row", 2 * k).astype(jnp.float32)
    return own


def apply_slots(
    panel, block_tiles, row_slot, set_slot, row_select, set_select, range_blocks, set_blocks
):
    width = panel.shape[1]
    gathered_set = lax.all_gather(panel, "row", axis=0, tiled=True).reshape(set_blocks, BS, width)
    picked_set = jnp.take(gathered_set, set_slot, axis=0)
    upper = jnp.einsum("sij,sjw->siw", block_tiles, picked_set, preferred_element_type=jnp.float32)
    upper_sum = jnp.einsum(
        "as,siw->aiw", row_select, upper, precision=lax.Precision.HIGHEST
    ).astype(jnp.bfloat16)
    own_upper = lax.psum_scatter(
        upper_sum.reshape(range_blocks * BS, width), "col", scatter_dimension=0, tiled=True
    ).astype(jnp.float32)
    gathered_range = lax.all_gather(panel, "col", axis=0, tiled=True).reshape(
        range_blocks, BS, width
    )
    picked_range = jnp.take(gathered_range, row_slot, axis=0)
    lower = jnp.einsum(
        "sji,sjw->siw", block_tiles, picked_range, preferred_element_type=jnp.float32
    )
    lower_sum = jnp.einsum(
        "bs,siw->biw", set_select, lower, precision=lax.Precision.HIGHEST
    ).astype(jnp.bfloat16)
    own_lower = lax.psum_scatter(
        lower_sum.reshape(set_blocks * BS, width), "row", scatter_dimension=0, tiled=True
    ).astype(jnp.float32)
    return own_upper + own_lower


def slot_operator(panel_blocks, block_tiles, tile_rows, tile_cols, owner_counts):
    n_rows = lax.axis_size("row")
    n_cols = lax.axis_size("col")
    row_index = lax.axis_index("row")
    slots = block_tiles.shape[0]
    range_blocks = panel_blocks * n_cols
    set_blocks = panel_blocks * n_rows
    row_slot = tile_rows - row_index * range_blocks
    shard_of = tile_cols // panel_blocks
    set_slot = shard_of // n_cols * panel_blocks + tile_cols % panel_blocks
    live_slots = jnp.arange(slots, dtype=jnp.int32) < owner_counts[0]
    row_select = (
        (row_slot[None, :] == jnp.arange(range_blocks, dtype=jnp.int32)[:, None])
        & live_slots[None, :]
    ).astype(jnp.float32)
    set_select = (
        (set_slot[None, :] == jnp.arange(set_blocks, dtype=jnp.int32)[:, None])
        & live_slots[None, :]
    ).astype(jnp.float32)

    def operate(panel):
        return apply_slots(
            panel, block_tiles, row_slot, set_slot, row_select, set_select, range_blocks, set_blocks
        )

    return operate


def is_dense(n_rows, n_cols, panel_blocks, slots):
    return (
        power_of_two(n_rows)
        and power_of_two(n_cols)
        and n_rows >= 4
        and n_cols >= 2
        and panel_blocks % 2 == 0
        and panel_blocks * n_cols * panel_blocks * n_rows <= 2 * slots
    )


def per_device(vector_panel, block_tiles, tile_rows, tile_cols, owner_counts):
    n_rows = lax.axis_size("row")
    n_cols = lax.axis_size("col")
    panel_blocks = vector_panel.shape[0] // BS
    if is_dense(n_rows, n_cols, panel_blocks, block_tiles.shape[0]):
        table = slot_table(
            n_rows, n_cols, panel_blocks, tile_rows, tile_cols, owner_counts
        )
        matrix = densify(panel_blocks * n_cols * BS, panel_blocks * n_rows * BS, table, block_tiles)
        matrix_t = transpose(matrix)
        operate = functools.partial(apply_dense, matrix=matrix, matrix_t=matrix_t)
    else:
        operate = slot_operator(panel_blocks, block_tiles, tile_rows, tile_cols, owner_counts)

    start_f = vector_panel.astype(jnp.float32)
    hx = operate(vector_panel)
    first_step = ((hx - center_shift * start_f) / half_width).astype(jnp.bfloat16)
    first_f = first_step.astype(jnp.float32)
    hfirst = operate(first_step)
    filtered = 2.0 * (hfirst - center_shift * first_f) / half_width - start_f
    return filtered.astype(jnp.bfloat16)


def solution(mesh):
    in_specs = (
        P(("row", "col"), None),
        P(("row", "col"), None, None),
        P(("row", "col")),
        P(("row", "col")),
        P(("row", "col")),
    )
    out_specs = P(("row", "col"), None)
    step = jax.shard_map(
        per_device, mesh=mesh, in_specs=in_specs, out_specs=out_specs, check_vma=False
    )

    def run(vector_panel, block_tiles, tile_rows, tile_cols, owner_counts):
        args = (vector_panel, block_tiles, tile_rows, tile_cols, owner_counts)
        return step(*args)

    return run
```

```python
import functools

import jax
import jax.numpy as jnp
from jax import lax
from jax.experimental import pallas as pl
from jax.experimental.pallas import tpu as pltpu
from jax.sharding import PartitionSpec as P


BS = 128
MIB = 2**20


center_shift = 0.25
half_width = 1.25


def power_of_two(n):
    return n & (n - 1) == 0


def slot_table(n_rows, n_cols, panel_blocks, tile_rows, tile_cols, owner_counts):
    slots = tile_rows.shape[0]
    range_blocks = panel_blocks * n_cols
    set_blocks = panel_blocks * n_rows
    p = lax.axis_index("row")
    q = lax.axis_index("col")
    row = tile_rows - p * range_blocks
    row_at = ((row // panel_blocks) ^ q) * panel_blocks + row % panel_blocks
    relative = (tile_cols // range_blocks) ^ p
    unit = (relative % 2) * (n_rows // 2) + relative // 2
    place = row_at * set_blocks + unit * panel_blocks + tile_cols % panel_blocks
    slot = jnp.arange(slots, dtype=jnp.int32)
    place = jnp.where(slot < owner_counts[0], place, -1)
    blocks = jnp.arange(range_blocks * set_blocks, dtype=jnp.int32)
    return jnp.min(jnp.where(place[None, :] == blocks[:, None], slot[None, :], slots), axis=1)


def densify_kernel(table, tiles_ref, a_ref):
    slots = tiles_ref.shape[0]
    set_blocks = a_ref.shape[1] // BS

    def fill(r, carry):
        for c in range(set_blocks):
            s = table[r * set_blocks + c]
            tile = tiles_ref[jnp.minimum(s, slots - 1)]
            tile = jnp.where(s < slots, tile, jnp.zeros_like(tile))
            a_ref[pl.ds(pl.multiple_of(r * BS, BS), BS), c * BS : (c + 1) * BS] = tile
        return carry

    lax.fori_loop(0, a_ref.shape[0] // BS, fill, 0)


def densify(height, breadth, table, block_tiles):
    vmem = pl.BlockSpec(memory_space=pltpu.VMEM)
    return pl.pallas_call(
        densify_kernel,
        out_shape=jax.ShapeDtypeStruct((height, breadth), block_tiles.dtype),
        in_specs=[pl.BlockSpec(memory_space=pltpu.SMEM), vmem],
        out_specs=vmem,
        compiler_params=pltpu.CompilerParams(vmem_limit_bytes=16 * MIB),
        cost_estimate=pl.CostEstimate(
            flops=0, transcendentals=0, bytes_accessed=2 * (block_tiles.size + height * breadth)
        ),
        name="densify",
    )(table, block_tiles)


def transpose_kernel(a_ref, at_ref):
    def fill(r, carry):
        rows = pl.ds(pl.multiple_of(r * BS, BS), BS)
        for c in range(a_ref.shape[1] // BS):
            at_ref[c * BS : (c + 1) * BS, rows] = a_ref[rows, c * BS : (c + 1) * BS].T
        return carry

    lax.fori_loop(0, a_ref.shape[0] // BS, fill, 0)


def transpose(matrix):
    height, breadth = matrix.shape
    vmem = pl.BlockSpec(memory_space=pltpu.VMEM)
    return pl.pallas_call(
        transpose_kernel,
        out_shape=jax.ShapeDtypeStruct((breadth, height), matrix.dtype),
        in_specs=[vmem],
        out_specs=vmem,
        compiler_params=pltpu.CompilerParams(vmem_limit_bytes=16 * MIB),
        cost_estimate=pl.CostEstimate(
            flops=0, transcendentals=0, bytes_accessed=4 * height * breadth
        ),
        name="mirror",
    )(matrix)


def product_kernel(n_in, starts, left, added, m_ref, *refs):
    panels, outs = refs[:n_in], refs[n_in + added :]
    for start, out in zip(starts, outs):
        for top in range(0, out.shape[0], 256):
            done = start + top
            total = refs[n_in][done : done + 256, :] if added else None
            at = left
            for panel in panels:
                rows = panel.shape[0]
                term = jnp.dot(
                    m_ref[done : done + 256, at : at + rows],
                    panel[...],
                    preferred_element_type=jnp.float32,
                )
                total = term if total is None else total + term
                at += rows
            out[top : top + 256, :] = total.astype(out.dtype)


def product(matrix, panels, pieces, left=0, added=None, dtype=jnp.bfloat16):
    width = panels[0].shape[1]
    depth = sum(panel.shape[0] for panel in panels)
    height = sum(rows for _, rows in pieces)
    extra = [] if added is None else [added]
    vmem = pl.BlockSpec(memory_space=pltpu.VMEM)
    return pl.pallas_call(
        functools.partial(
            product_kernel, len(panels), [first for first, _ in pieces], left, len(extra)
        ),
        out_shape=tuple(jax.ShapeDtypeStruct((rows, width), dtype) for _, rows in pieces),
        in_specs=[vmem] * (1 + len(panels) + len(extra)),
        out_specs=tuple(vmem for _ in pieces),
        compiler_params=pltpu.CompilerParams(vmem_limit_bytes=16 * MIB),
        cost_estimate=pl.CostEstimate(
            flops=2 * height * depth * width,
            transcendentals=0,
            bytes_accessed=2 * (height * (depth + width) + depth * width),
        ),
    )(matrix, *panels, *extra)


def swap(x, axis, j):
    return lax.ppermute(x, axis, [(i, i ^ j) for i in range(lax.axis_size(axis))])


def hops(j):
    masks = []
    while j:
        masks.append((1 << j.bit_length()) - 1)
        j ^= masks[-1]
    return masks


def apply_dense(panel, matrix, matrix_t):
    n_rows = lax.axis_size("row")
    n_cols = lax.axis_size("col")
    rows, width = panel.shape
    half = n_rows // 2
    by_hops = sorted(range(1, n_cols), key=lambda j: (len(hops(j)), -j))

    range_panels = [panel] + [None] * (n_cols - 1)
    for j in by_hops:
        last = hops(j)[-1]
        range_panels[j] = swap(range_panels[j ^ last], "col", last)
    near = [panel] + [swap(panel, "row", 2 * k) for k in range(1, half)]
    far = swap(jnp.concatenate(near), "row", 1)
    (begun,) = product(matrix, near, [(0, n_cols * rows)], dtype=jnp.float32)
    upper = [None] * n_cols
    early = [j for j in by_hops if len(hops(j)) == len(hops(by_hops[-1]))]
    late = [j for j in range(n_cols) if j not in early]
    for units in (early, late):
        pieces = [(j * rows, rows) for j in units]
        done = product(matrix, [far], pieces, half * rows, begun)
        for j, unit in zip(units, done):
            upper[j] = unit
    for j in reversed(by_hops):
        last = hops(j)[-1]
        part = swap(upper[j].astype(jnp.bfloat16), "col", last)
        upper[j ^ last] = upper[j ^ last].astype(jnp.float32) + part.astype(jnp.float32)
    own = upper[0].astype(jnp.float32)
    (give,) = product(matrix_t, range_panels, [(half * rows, half * rows)])
    (keep,) = product(matrix_t, range_panels, [(0, half * rows)])
    paired = keep.astype(jnp.float32) + swap(give, "row", 1).astype(jnp.float32)
    paired = paired.reshape(half, rows, width)
    own += paired[0]
    for k in range(1, half):
        share = paired[k].astype(jnp.bfloat16)
        own += swap(share, "row", 2 * k).astype(jnp.float32)
    return own


def apply_slots(
    panel, block_tiles, row_slot, set_slot, row_select, set_select, range_blocks, set_blocks
):
    width = panel.shape[1]
    gathered_set = lax.all_gather(panel, "row", axis=0, tiled=True).reshape(set_blocks, BS, width)
    picked_set = jnp.take(gathered_set, set_slot, axis=0)
    upper = jnp.einsum("sij,sjw->siw", block_tiles, picked_set, preferred_element_type=jnp.float32)
    upper_sum = jnp.einsum(
        "as,siw->aiw", row_select, upper, precision=lax.Precision.HIGHEST
    ).astype(jnp.bfloat16)
    own_upper = lax.psum_scatter(
        upper_sum.reshape(range_blocks * BS, width), "col", scatter_dimension=0, tiled=True
    ).astype(jnp.float32)
    gathered_range = lax.all_gather(panel, "col", axis=0, tiled=True).reshape(
        range_blocks, BS, width
    )
    picked_range = jnp.take(gathered_range, row_slot, axis=0)
    lower = jnp.einsum(
        "sji,sjw->siw", block_tiles, picked_range, preferred_element_type=jnp.float32
    )
    lower_sum = jnp.einsum(
        "bs,siw->biw", set_select, lower, precision=lax.Precision.HIGHEST
    ).astype(jnp.bfloat16)
    own_lower = lax.psum_scatter(
        lower_sum.reshape(set_blocks * BS, width), "row", scatter_dimension=0, tiled=True
    ).astype(jnp.float32)
    return own_upper + own_lower


def slot_operator(panel_blocks, block_tiles, tile_rows, tile_cols, owner_counts):
    n_rows = lax.axis_size("row")
    n_cols = lax.axis_size("col")
    row_index = lax.axis_index("row")
    slots = block_tiles.shape[0]
    range_blocks = panel_blocks * n_cols
    set_blocks = panel_blocks * n_rows
    row_slot = tile_rows - row_index * range_blocks
    shard_of = tile_cols // panel_blocks
    set_slot = shard_of // n_cols * panel_blocks + tile_cols % panel_blocks
    live_slots = jnp.arange(slots, dtype=jnp.int32) < owner_counts[0]
    row_select = (
        (row_slot[None, :] == jnp.arange(range_blocks, dtype=jnp.int32)[:, None])
        & live_slots[None, :]
    ).astype(jnp.float32)
    set_select = (
        (set_slot[None, :] == jnp.arange(set_blocks, dtype=jnp.int32)[:, None])
        & live_slots[None, :]
    ).astype(jnp.float32)

    def operate(panel):
        return apply_slots(
            panel, block_tiles, row_slot, set_slot, row_select, set_select, range_blocks, set_blocks
        )

    return operate


def is_dense(n_rows, n_cols, panel_blocks, slots):
    return (
        power_of_two(n_rows)
        and power_of_two(n_cols)
        and n_rows >= 4
        and n_cols >= 2
        and panel_blocks % 2 == 0
        and panel_blocks * n_cols * panel_blocks * n_rows <= 2 * slots
    )


def per_device(vector_panel, block_tiles, tile_rows, tile_cols, owner_counts):
    n_rows = lax.axis_size("row")
    n_cols = lax.axis_size("col")
    panel_blocks = vector_panel.shape[0] // BS
    if is_dense(n_rows, n_cols, panel_blocks, block_tiles.shape[0]):
        table = slot_table(
            n_rows, n_cols, panel_blocks, tile_rows, tile_cols, owner_counts
        )
        matrix = densify(panel_blocks * n_cols * BS, panel_blocks * n_rows * BS, table, block_tiles)
        matrix_t = transpose(matrix)
        operate = functools.partial(apply_dense, matrix=matrix, matrix_t=matrix_t)
    else:
        operate = slot_operator(panel_blocks, block_tiles, tile_rows, tile_cols, owner_counts)

    start_f = vector_panel.astype(jnp.float32)
    hx = operate(vector_panel)
    first_step = ((hx - center_shift * start_f) / half_width).astype(jnp.bfloat16)
    first_f = first_step.astype(jnp.float32)
    hfirst = operate(first_step)
    filtered = 2.0 * (hfirst - center_shift * first_f) / half_width - start_f
    return filtered.astype(jnp.bfloat16)


def solution(mesh):
    in_specs = (
        P(("row", "col"), None),
        P(("row", "col"), None, None),
        P(("row", "col")),
        P(("row", "col")),
        P(("row", "col")),
    )
    out_specs = P(("row", "col"), None)
    step = jax.shard_map(
        per_device, mesh=mesh, in_specs=in_specs, out_specs=out_specs, check_vma=False
    )

    def run(vector_panel, block_tiles, tile_rows, tile_cols, owner_counts):
        args = (vector_panel, block_tiles, tile_rows, tile_cols, owner_counts)
        return step(*args)

    return run
```

```python
import functools

import jax
import jax.numpy as jnp
from jax import lax
from jax.experimental import pallas as pl
from jax.experimental.pallas import tpu as pltpu
from jax.sharding import PartitionSpec as P


BS = 128
MIB = 2**20


center_shift = 0.25
half_width = 1.25


def power_of_two(n):
    return n & (n - 1) == 0


def slot_table(n_rows, n_cols, panel_blocks, tile_rows, tile_cols, owner_counts):
    slots = tile_rows.shape[0]
    range_blocks = panel_blocks * n_cols
    set_blocks = panel_blocks * n_rows
    p = lax.axis_index("row")
    q = lax.axis_index("col")
    row = tile_rows - p * range_blocks
    row_at = ((row // panel_blocks) ^ q) * panel_blocks + row % panel_blocks
    relative = (tile_cols // range_blocks) ^ p
    unit = (relative % 2) * (n_rows // 2) + relative // 2
    place = row_at * set_blocks + unit * panel_blocks + tile_cols % panel_blocks
    slot = jnp.arange(slots, dtype=jnp.int32)
    place = jnp.where(slot < owner_counts[0], place, -1)
    blocks = jnp.arange(range_blocks * set_blocks, dtype=jnp.int32)
    return jnp.min(jnp.where(place[None, :] == blocks[:, None], slot[None, :], slots), axis=1)


def densify_kernel(table, tiles_ref, a_ref):
    slots = tiles_ref.shape[0]
    set_blocks = a_ref.shape[1] // BS

    def fill(r, carry):
        for c in range(set_blocks):
            s = table[r * set_blocks + c]
            tile = tiles_ref[jnp.minimum(s, slots - 1)]
            tile = jnp.where(s < slots, tile, jnp.zeros_like(tile))
            a_ref[pl.ds(pl.multiple_of(r * BS, BS), BS), c * BS : (c + 1) * BS] = tile
        return carry

    lax.fori_loop(0, a_ref.shape[0] // BS, fill, 0)


def densify(height, breadth, table, block_tiles):
    vmem = pl.BlockSpec(memory_space=pltpu.VMEM)
    return pl.pallas_call(
        densify_kernel,
        out_shape=jax.ShapeDtypeStruct((height, breadth), block_tiles.dtype),
        in_specs=[pl.BlockSpec(memory_space=pltpu.SMEM), vmem],
        out_specs=vmem,
        compiler_params=pltpu.CompilerParams(vmem_limit_bytes=16 * MIB),
        cost_estimate=pl.CostEstimate(
            flops=0, transcendentals=0, bytes_accessed=2 * (block_tiles.size + height * breadth)
        ),
        name="densify",
    )(table, block_tiles)


def transpose_kernel(a_ref, at_ref):
    def fill(r, carry):
        rows = pl.ds(pl.multiple_of(r * BS, BS), BS)
        for c in range(a_ref.shape[1] // BS):
            at_ref[c * BS : (c + 1) * BS, rows] = a_ref[rows, c * BS : (c + 1) * BS].T
        return carry

    lax.fori_loop(0, a_ref.shape[0] // BS, fill, 0)


def transpose(matrix):
    height, breadth = matrix.shape
    vmem = pl.BlockSpec(memory_space=pltpu.VMEM)
    return pl.pallas_call(
        transpose_kernel,
        out_shape=jax.ShapeDtypeStruct((breadth, height), matrix.dtype),
        in_specs=[vmem],
        out_specs=vmem,
        compiler_params=pltpu.CompilerParams(vmem_limit_bytes=16 * MIB),
        cost_estimate=pl.CostEstimate(
            flops=0, transcendentals=0, bytes_accessed=4 * height * breadth
        ),
        name="mirror",
    )(matrix)


def product_kernel(n_in, starts, left, added, m_ref, *refs):
    panels, outs = refs[:n_in], refs[n_in + added :]
    for start, out in zip(starts, outs):
        for top in range(0, out.shape[0], 256):
            done = start + top
            total = refs[n_in][done : done + 256, :] if added else None
            at = left
            for panel in panels:
                rows = panel.shape[0]
                term = jnp.dot(
                    m_ref[done : done + 256, at : at + rows],
                    panel[...],
                    preferred_element_type=jnp.float32,
                )
                total = term if total is None else total + term
                at += rows
            out[top : top + 256, :] = total.astype(out.dtype)


def product(matrix, panels, pieces, left=0, added=None, dtype=jnp.bfloat16):
    width = panels[0].shape[1]
    depth = sum(panel.shape[0] for panel in panels)
    height = sum(rows for _, rows in pieces)
    extra = [] if added is None else [added]
    vmem = pl.BlockSpec(memory_space=pltpu.VMEM)
    return pl.pallas_call(
        functools.partial(
            product_kernel, len(panels), [first for first, _ in pieces], left, len(extra)
        ),
        out_shape=tuple(jax.ShapeDtypeStruct((rows, width), dtype) for _, rows in pieces),
        in_specs=[vmem] * (1 + len(panels) + len(extra)),
        out_specs=tuple(vmem for _ in pieces),
        compiler_params=pltpu.CompilerParams(vmem_limit_bytes=16 * MIB),
        cost_estimate=pl.CostEstimate(
            flops=2 * height * depth * width,
            transcendentals=0,
            bytes_accessed=2 * (height * (depth + width) + depth * width),
        ),
    )(matrix, *panels, *extra)


def swap(x, axis, j):
    return lax.ppermute(x, axis, [(i, i ^ j) for i in range(lax.axis_size(axis))])


def hops(j):
    masks = []
    while j:
        masks.append((1 << j.bit_length()) - 1)
        j ^= masks[-1]
    return masks


def apply_dense(panel, matrix, matrix_t):
    n_rows = lax.axis_size("row")
    n_cols = lax.axis_size("col")
    rows, _ = panel.shape
    half = n_rows // 2
    by_hops = sorted(range(1, n_cols), key=lambda j: (len(hops(j)), -j))

    range_panels = [panel] + [None] * (n_cols - 1)
    for j in by_hops:
        last = hops(j)[-1]
        range_panels[j] = swap(range_panels[j ^ last], "col", last)
    near = [panel] + [swap(panel, "row", 2 * k) for k in range(1, half)]
    far = swap(jnp.concatenate(near), "row", 1)
    (begun,) = product(matrix, near, [(0, n_cols * rows)], dtype=jnp.float32)
    upper = [None] * n_cols
    early = [j for j in by_hops if len(hops(j)) == len(hops(by_hops[-1]))]
    late = [j for j in by_hops if j not in early]
    for units in (early, late, [0]):
        pieces = [(j * rows, rows) for j in units]
        done = product(matrix, [far], pieces, half * rows, begun)
        for j, unit in zip(units, done):
            upper[j] = unit
    for j in reversed(by_hops):
        last = hops(j)[-1]
        part = swap(upper[j].astype(jnp.bfloat16), "col", last)
        upper[j ^ last] = upper[j ^ last].astype(jnp.float32) + part.astype(jnp.float32)
    own = upper[0].astype(jnp.float32)
    (give,) = product(matrix_t, range_panels, [(half * rows, half * rows)])
    (keep,) = product(matrix_t, range_panels, [(rows, (half - 1) * rows)])
    (mine,) = product(matrix_t, range_panels, [(0, rows)])
    given = swap(give, "row", 1).astype(jnp.float32)
    paired = keep.astype(jnp.float32) + given[rows:]
    own += mine.astype(jnp.float32) + given[:rows]
    for k in range(1, half):
        share = paired[(k - 1) * rows : k * rows].astype(jnp.bfloat16)
        own += swap(share, "row", 2 * k).astype(jnp.float32)
    return own


def apply_slots(
    panel, block_tiles, row_slot, set_slot, row_select, set_select, range_blocks, set_blocks
):
    width = panel.shape[1]
    gathered_set = lax.all_gather(panel, "row", axis=0, tiled=True).reshape(set_blocks, BS, width)
    picked_set = jnp.take(gathered_set, set_slot, axis=0)
    upper = jnp.einsum("sij,sjw->siw", block_tiles, picked_set, preferred_element_type=jnp.float32)
    upper_sum = jnp.einsum(
        "as,siw->aiw", row_select, upper, precision=lax.Precision.HIGHEST
    ).astype(jnp.bfloat16)
    own_upper = lax.psum_scatter(
        upper_sum.reshape(range_blocks * BS, width), "col", scatter_dimension=0, tiled=True
    ).astype(jnp.float32)
    gathered_range = lax.all_gather(panel, "col", axis=0, tiled=True).reshape(
        range_blocks, BS, width
    )
    picked_range = jnp.take(gathered_range, row_slot, axis=0)
    lower = jnp.einsum(
        "sji,sjw->siw", block_tiles, picked_range, preferred_element_type=jnp.float32
    )
    lower_sum = jnp.einsum(
        "bs,siw->biw", set_select, lower, precision=lax.Precision.HIGHEST
    ).astype(jnp.bfloat16)
    own_lower = lax.psum_scatter(
        lower_sum.reshape(set_blocks * BS, width), "row", scatter_dimension=0, tiled=True
    ).astype(jnp.float32)
    return own_upper + own_lower


def slot_operator(panel_blocks, block_tiles, tile_rows, tile_cols, owner_counts):
    n_rows = lax.axis_size("row")
    n_cols = lax.axis_size("col")
    row_index = lax.axis_index("row")
    slots = block_tiles.shape[0]
    range_blocks = panel_blocks * n_cols
    set_blocks = panel_blocks * n_rows
    row_slot = tile_rows - row_index * range_blocks
    shard_of = tile_cols // panel_blocks
    set_slot = shard_of // n_cols * panel_blocks + tile_cols % panel_blocks
    live_slots = jnp.arange(slots, dtype=jnp.int32) < owner_counts[0]
    row_select = (
        (row_slot[None, :] == jnp.arange(range_blocks, dtype=jnp.int32)[:, None])
        & live_slots[None, :]
    ).astype(jnp.float32)
    set_select = (
        (set_slot[None, :] == jnp.arange(set_blocks, dtype=jnp.int32)[:, None])
        & live_slots[None, :]
    ).astype(jnp.float32)

    def operate(panel):
        return apply_slots(
            panel, block_tiles, row_slot, set_slot, row_select, set_select, range_blocks, set_blocks
        )

    return operate


def is_dense(n_rows, n_cols, panel_blocks, slots):
    return (
        power_of_two(n_rows)
        and power_of_two(n_cols)
        and n_rows >= 4
        and n_cols >= 2
        and panel_blocks % 2 == 0
        and panel_blocks * n_cols * panel_blocks * n_rows <= 2 * slots
    )


def per_device(vector_panel, block_tiles, tile_rows, tile_cols, owner_counts):
    n_rows = lax.axis_size("row")
    n_cols = lax.axis_size("col")
    panel_blocks = vector_panel.shape[0] // BS
    if is_dense(n_rows, n_cols, panel_blocks, block_tiles.shape[0]):
        table = slot_table(
            n_rows, n_cols, panel_blocks, tile_rows, tile_cols, owner_counts
        )
        matrix = densify(panel_blocks * n_cols * BS, panel_blocks * n_rows * BS, table, block_tiles)
        matrix_t = transpose(matrix)
        operate = functools.partial(apply_dense, matrix=matrix, matrix_t=matrix_t)
    else:
        operate = slot_operator(panel_blocks, block_tiles, tile_rows, tile_cols, owner_counts)

    start_f = vector_panel.astype(jnp.float32)
    hx = operate(vector_panel)
    first_step = ((hx - center_shift * start_f) / half_width).astype(jnp.bfloat16)
    first_f = first_step.astype(jnp.float32)
    hfirst = operate(first_step)
    filtered = 2.0 * (hfirst - center_shift * first_f) / half_width - start_f
    return filtered.astype(jnp.bfloat16)


def solution(mesh):
    in_specs = (
        P(("row", "col"), None),
        P(("row", "col"), None, None),
        P(("row", "col")),
        P(("row", "col")),
        P(("row", "col")),
    )
    out_specs = P(("row", "col"), None)
    step = jax.shard_map(
        per_device, mesh=mesh, in_specs=in_specs, out_specs=out_specs, check_vma=False
    )

    def run(vector_panel, block_tiles, tile_rows, tile_cols, owner_counts):
        args = (vector_panel, block_tiles, tile_rows, tile_cols, owner_counts)
        return step(*args)

    return run
```
